256 devices in a mesh: chan: 16 (over x, y), win: 16 (over z, core).
Axes of the slice: x: 4, y: 4, z: 8, core: 2. Of those that a mesh axis runs over, the one named last changes fastest.
Arguments:
- traces: float32 [16, 160, 48, 2048], P('win', 'chan'), may hold values from -54 to 54
- pair_blocks: int32 [48, 2], replicated, may hold values from 0 to 159, as said below
- pair_count: int32 [16], replicated, may hold values from 1 to 3, 32 in all
Outputs:
- stacks: float32 [64, 48, 2304], P('win', 'chan')
The draws below stay inside these ranges and needn't reach their ends.
Inputs may be any that keep to these rules, and one draw needn't show every extreme that they name: `pair_blocks`: the blocks of owner o's slots form a chain c_0, ..., c_3: slot 3 * o + k holds (c_k, c_k+1); c_k lies on index q + k of chan (block c lies on index c // 10) for some q of the owner, and 1 <= c_k+1 - c_k <= 16. `pair_count`: the counts sum to 32.
All inputs are finite; a program needn't handle non-finite values.
Results may differ from the reference program's by a relative error of at most 0.0041.
Values may be sent and summed in bfloat16 or wider, within the bound.
A program may use at most 64 MiB of HBM per device.

```python
import math
import jax
import jax.numpy as jnp
import numpy as np
from jax import lax

CH = 48
TS = 2048
LAGS = 64
BLK_DEV = 10
SPAN = 16
P_CAP = 3
BLOCKS = 160
OWNERS = 16
PSLOTS = 48
PAIRS_LIVE = 32
WINDOWS = 16


def draw_traces(key, part):
    scale_key, offset_key, noise_key = jax.random.split(key, 3)
    shape = (WINDOWS, BLOCKS, CH, TS)
    channel_scale = jnp.exp(jax.random.uniform(scale_key, (1, BLOCKS, CH, 1), jnp.float32, 0.0, math.log(10.0)))
    offsets = jax.random.uniform(offset_key, (WINDOWS, BLOCKS, CH, 1), jnp.float32, -4.0, 4.0)
    noise = jax.random.normal(noise_key, shape, jnp.float32)
    noise = jnp.clip(noise, -5.0, 5.0)
    return (offsets + channel_scale * noise).astype(jnp.float32)


def draw_pair_blocks(key, part):
    anchor_key, start_key, move_key = jax.random.split(key, 3)
    anchors = jax.random.randint(anchor_key, (OWNERS,), 0, OWNERS - P_CAP, jnp.int32)
    starts = jax.random.randint(start_key, (OWNERS,), 0, BLK_DEV, jnp.int32)
    moves = jax.random.randint(move_key, (OWNERS, P_CAP), 1 - BLK_DEV, SPAN - BLK_DEV + 1, jnp.int32)
    anchors = anchors.at[0].set(0).at[OWNERS - 1].set(OWNERS - P_CAP - 1)
    starts = starts.at[0].set(0).at[OWNERS - 1].set(BLK_DEV - 1)
    moves = moves.at[0, 0].set(SPAN - BLK_DEV).at[OWNERS - 1].set(0)
    within = [starts]
    for step_number in range(P_CAP):
        within.append(jnp.clip(within[-1] + moves[:, step_number], 0, BLK_DEV - 1))
    chain = jnp.stack([(anchors + step_number) * BLK_DEV + within[step_number] for step_number in range(P_CAP + 1)], axis=1)
    rows = jnp.stack([chain[:, :-1], chain[:, 1:]], axis=2)
    return rows.reshape(OWNERS * P_CAP, 2).astype(jnp.int32)


def profile(amount, total, limit, slope):
    loads = [(1 << 20) // math.isqrt(standing ** slope) + 1 for standing in range(2, amount + 1)]
    surplus, holding = total - limit - (amount - 1), [1] * (amount - 1)
    while surplus > 0:
        candidates = [i for i in range(amount - 1) if holding[i] < limit]
        pool, remaining = sum([loads[i] for i in candidates]), surplus
        for i in candidates:
            addition = min(limit - holding[i], max(1, remaining * loads[i] // pool), surplus)
            holding[i] = holding[i] + addition
            surplus = surplus - addition
    return np.array([limit] + holding)


def ragged(key, amount, total, limit, skew):
    if amount == 2:
        one = jax.random.randint(key, (), max(1, total - limit), min(limit, total - 1) + 1)
        return jnp.stack([one, total - one])
    tallies = jnp.asarray(profile(amount, total, limit, skew), jnp.int32)
    couples = (amount - 1) // 2
    donor, receiver = tallies[1:1 + 2 * couples:2], tallies[2:2 + 2 * couples:2]
    room = jnp.minimum(donor - 1, limit - receiver)
    moved = jax.random.randint(jax.random.fold_in(key, 1), (couples,), 0, 1 << 20) % (room + 1)
    tallies = tallies.at[1:1 + 2 * couples:2].set(donor - moved).at[2:2 + 2 * couples:2].set(receiver + moved)
    return tallies[jax.random.permutation(jax.random.fold_in(key, 2), amount)]


def setup_inputs(seed: int = 0) -> dict:
    seeds = jax.random.split(jax.random.key(seed), 4)
    return {
        "traces": draw_traces(jax.random.fold_in(seeds[3], 71), 0),
        "pair_blocks": draw_pair_blocks(jax.random.fold_in(seeds[3], 71), 0),
        "pair_count": ragged(seeds[2], OWNERS, PAIRS_LIVE, P_CAP, 2).astype(jnp.int32),
    }


EPS = 1e-06

def whiten(signal):
    centred = signal - lax.optimization_barrier(jnp.mean(signal, axis=-1, keepdims=True))
    power = lax.optimization_barrier(jnp.mean(centred * centred, axis=-1, keepdims=True))
    return (centred * lax.rsqrt(power + EPS)).astype(jnp.bfloat16)

def correlate(left_side, right_side):
    half_lags = LAGS // 2
    padded = jnp.pad(right_side, ((0, 0), (0, 0), (half_lags, half_lags)))
    width = math.gcd(LAGS, 4)
    left_wide = left_side.astype(jnp.float32)

    def lag_block(first_lag):
        shifted = jnp.stack([lax.dynamic_slice_in_dim(padded, first_lag + offset_lag, TS, axis=2) for offset_lag in range(width)], axis=1)
        return jnp.einsum('wit,wgjt->gij', left_wide, shifted.astype(jnp.float32))
    firsts = (jnp.arange(LAGS // width) * width).astype(jnp.int32)
    return lax.map(lag_block, firsts).reshape(LAGS, CH * CH)

def reference(traces, pair_blocks, pair_count):
    norm_scale = 1.0 / math.sqrt(TS * WINDOWS)

    def one_slot(row):
        first_block = pair_blocks[row, 0]
        second_block = pair_blocks[row, 1]
        owner = row // P_CAP
        slot_number = row % P_CAP
        live_mask = jnp.where(slot_number < pair_count[owner], 1.0, 0.0).astype(jnp.float32)
        left_side = whiten(jnp.take(traces, first_block, axis=1))
        right_side = whiten(jnp.take(traces, second_block, axis=1))
        return correlate(left_side, right_side) * (norm_scale * live_mask)
    stacked = lax.map(one_slot, jnp.arange(PSLOTS, dtype=jnp.int32))
    return jnp.transpose(stacked, (1, 0, 2))
```

```python
import functools
import math

import jax
import jax.numpy as jnp
from jax import lax
from jax.experimental import pallas as pl
from jax.experimental.pallas import tpu as pltpu
from jax.sharding import PartitionSpec as P

LAGS = 64
P_CAP = 3
EPS = 1e-06
TIERS = ((2, 4), (3, 4), (4, 6))
BF16 = jnp.bfloat16
F32 = jnp.float32


def whiten(signal):
    centred = signal - jnp.mean(signal, axis=-1, keepdims=True)
    power = jnp.mean(centred * centred, axis=-1, keepdims=True)
    return (centred * lax.rsqrt(power + EPS)).astype(BF16)


def fetch_blocks(traces, requests, per_peer, my_index, blocks_here):
    owners = requests.shape[0]
    home_index = requests // blocks_here
    is_local = home_index == my_index
    slot_rank = jnp.cumsum(is_local.astype(jnp.int32), axis=1) - 1
    chosen = is_local[:, :, None] & (
        slot_rank[:, :, None] == jnp.arange(per_peer, dtype=jnp.int32)[None, None, :]
    )
    local_block = jnp.sum(
        jnp.where(chosen, requests[:, :, None] - my_index * blocks_here, 0), axis=1
    ).reshape(-1)
    is_valid = jnp.any(chosen, axis=1).reshape(1, -1, 1, 1)
    owner_ids = jnp.arange(owners, dtype=jnp.int32)
    my_requests = jnp.sum(jnp.where((owner_ids == my_index)[:, None], requests, 0), axis=0)
    my_home = my_requests // blocks_here
    request_total = my_requests.shape[0]
    request_ids = jnp.arange(request_total, dtype=jnp.int32)
    earlier = request_ids[None, :] < request_ids[:, None]
    my_rank = jnp.sum((earlier & (my_home[None, :] == my_home[:, None])).astype(jnp.int32), axis=1)
    position = my_home * per_peer + my_rank
    outgoing = jnp.where(
        is_valid, jnp.take(traces, local_block, axis=1), jnp.zeros((), jnp.float32)
    )
    incoming = lax.all_to_all(outgoing, "chan", split_axis=1, concat_axis=1, tiled=True)
    return whiten(jnp.take(incoming, position, axis=1))


def general_path(traces, pair_blocks, pair_count):
    owners = lax.axis_size("chan")
    my_index = lax.axis_index("chan")
    blocks_here = traces.shape[1]
    channels = traces.shape[2]
    samples = traces.shape[3]
    windows = traces.shape[0] * lax.axis_size("win")
    norm_scale = 1.0 / math.sqrt(samples * windows)
    pair_table = pair_blocks.reshape(owners, P_CAP, 2)
    owner_ids = jnp.arange(owners, dtype=jnp.int32)
    mine_row = owner_ids == my_index
    my_count = jnp.sum(jnp.where(mine_row, pair_count, 0))
    requests = jnp.concatenate([pair_table[:, :, 0], pair_table[:, P_CAP - 1 :, 1]], axis=1)
    live_mask = (jnp.arange(P_CAP, dtype=jnp.int32) < my_count).astype(jnp.float32)
    fetched = fetch_blocks(traces, requests, 1, my_index, blocks_here)
    left_side = jnp.stack([fetched[:, row] for row in range(P_CAP)], axis=1)
    right_side = jnp.stack([fetched[:, row + 1] for row in range(P_CAP)], axis=1)
    half_lags = LAGS // 2
    padded = jnp.pad(right_side, ((0, 0), (0, 0), (0, 0), (half_lags, half_lags)))
    weights = live_mask * norm_scale
    width = 8

    def lag_block(first_lag):
        shifted = jnp.stack(
            [
                lax.dynamic_slice_in_dim(padded, first_lag + offset_lag, samples, axis=3)
                for offset_lag in range(width)
            ],
            axis=2,
        )
        product = jnp.einsum(
            "wpit,wpgjt->gpij", left_side, shifted, preferred_element_type=jnp.float32
        )
        return product.reshape(width, P_CAP, channels * channels) * weights[None, :, None]

    firsts = jnp.arange(LAGS // width, dtype=jnp.int32) * width
    return lax.psum_scatter(
        lax.map(lag_block, firsts).reshape(LAGS, P_CAP, channels * channels),
        "win",
        scatter_dimension=0,
        tiled=True,
    )


def kernel(
    n, S, tab, wt, traces, out,
    raw, abuf, bbuf, ysend, yfirst, yrest, xsend, xrecv, acc, zsend, zrecv, own, fsend, frecv,
    load_sem, ys_sem, yr_sem, xs_sem, xr_sem, zs_sem, zr_sem, fs_sem, fr_sem,
):
    n_chan = lax.axis_size("chan")
    n_z = lax.axis_size("win") // 2
    p = lax.axis_index("chan")
    w = lax.axis_index("win")
    z = w // 2
    c = w % 2
    B, CH, TS = raw.shape
    half = CH // 2
    K = abuf.shape[1]

    loads = [pltpu.make_async_copy(traces.at[0, b], raw.at[b], load_sem.at[b]) for b in range(B)]
    for copy in loads:
        copy.start()

    barrier = pltpu.get_barrier_semaphore()
    for d in range(1, n_chan):
        pl.semaphore_signal(
            barrier, inc=1, device_id={"chan": lax.rem(p + d, n_chan)}, device_id_type=MESH
        )
    for d in range(1, n_z):
        pl.semaphore_signal(
            barrier, inc=1, device_id={"win": lax.rem(z + d, n_z) * 2 + c}, device_id_type=MESH
        )
    pl.semaphore_signal(barrier, inc=1, device_id={"win": z * 2 + 1 - c}, device_id_type=MESH)

    bbuf[:, 4 * CH :, :] = jnp.zeros((2, bbuf.shape[1] - 4 * CH, K), BF16)
    for copy in loads:
        copy.wait()

    def y_copy(side, s):
        dst = yfirst.at[side] if s == 0 else yrest.at[side * (n - 1) + s - 1]
        peer = lax.rem(p + (n_chan - 1 if side == 0 else 1), n_chan)
        return pltpu.make_async_remote_copy(
            src_ref=ysend.at[side, s], dst_ref=dst,
            send_sem=ys_sem.at[side, s], recv_sem=yr_sem.at[side, s],
            device_id={"chan": peer}, device_id_type=MESH,
        )

    for s in range(n):
        for side in range(2):
            block = tab[side * n + s]
            for g in range(0, CH, 16):
                ysend[side, s, g : g + 16, :] = whiten(raw[block, g : g + 16, :])
            if s == 0 and side == 0:
                pl.semaphore_wait(barrier, n_chan - 1 + n_z)
            y_copy(side, s).start()

    zeros = jnp.zeros((16, K - TS), BF16)
    low = lax.broadcasted_iota(jnp.int32, (half, 128), 1) < 64

    def fold(C, write):
        for zz in range(n_z):
            top = C[zz * CH : zz * CH + half, :]
            bottom = C[zz * CH + half : (zz + 1) * CH, :]
            r0 = pltpu.roll(bottom[:, 0:128], 64, 1)
            r1 = pltpu.roll(bottom[:, 128:256], 64, 1)
            write(zz, 0, top[:, 0:128])
            write(zz, 1, jnp.where(low, top[:, 128:256], r0))
            write(zz, 2, jnp.where(low, r0, r1))

    def dot(index):
        return lax.dot_general(
            abuf[...], bbuf[index], (((1,), (1,)), ((), ())), preferred_element_type=F32
        )

    def x_copy(s):
        return pltpu.make_async_remote_copy(
            src_ref=xsend.at[s], dst_ref=xrecv.at[s],
            send_sem=xs_sem.at[s], recv_sem=xr_sem.at[s],
            device_id={"win": z * 2 + 1 - c}, device_id_type=MESH,
        )

    def z_copy(s, d):
        peer = lax.rem(z + d, n_z)
        return pltpu.make_async_remote_copy(
            src_ref=zsend.at[s, peer], dst_ref=zrecv.at[s, d],
            send_sem=zs_sem.at[s, d], recv_sem=zr_sem.at[s, d],
            device_id={"win": peer * 2 + c}, device_id_type=MESH,
        )

    def f_copy(s, d):
        return pltpu.make_async_remote_copy(
            src_ref=fsend.at[s], dst_ref=frecv.at[d * S + s],
            send_sem=fs_sem.at[s, d], recv_sem=fr_sem.at[s, d],
            device_id={"chan": lax.rem(p + d, n_chan)}, device_id_type=MESH,
        )

    for s in range(S):
        block = tab[2 * n + s]
        if s < 2:
            y_copy(s, 0).wait_recv()
        elif s == 2:
            for side in range(2):
                for t in range(1, n):
                    y_copy(side, t).wait_recv()
        for g in range(0, CH, 16):
            mine = whiten(raw[block, g : g + 16, :])
            if s == 0:
                left, right = mine, yfirst[0, g : g + 16, :]
            elif s == 1:
                left, right = yfirst[1, g : g + 16, :], mine
            else:
                other = yrest[tab[2 * n + S + s], g : g + 16, :]
                is_left = tab[2 * n + 2 * S + s] == 1
                left = jnp.where(is_left, mine, other)
                right = jnp.where(is_left, other, mine)
            left = jnp.concatenate([left, zeros], axis=1)
            right = jnp.concatenate([right, zeros], axis=1)
            for zz in range(n_z):
                row = zz * CH + g
                abuf[row : row + 16, :] = pltpu.roll(left, (8 * zz - 25) % K, 1)
            for u in range(8):
                row = (u % 4) * CH + g
                bbuf[u // 4, row : row + 16, :] = pltpu.roll(right, 7 - u, 1)

        def write_send(zz, t, value):
            xsend[s, zz, :, t * 128 : (t + 1) * 128] = value.astype(BF16)

        def write_acc(zz, t, value):
            acc[zz, :, t * 128 : (t + 1) * 128] = value

        fold(dot(1 - c), write_send)
        x_copy(s).start()
        fold(dot(c), write_acc)
        x_copy(s).wait_recv()
        for zz in range(n_z):
            zsend[s, zz] = (acc[zz] + xrecv[s, zz].astype(F32)).astype(BF16)
        own[s] = acc[z] + xrecv[s, z].astype(F32)
        for d in range(1, n_z):
            z_copy(s, d).start()

    for s in range(S):
        total = own[s]
        for d in range(1, n_z):
            z_copy(s, d).wait_recv()
            total = total + zrecv[s, d].astype(F32)
        total = total.astype(BF16)
        fsend[s] = total
        for d in range(1, n_chan):
            f_copy(s, d).start()
        frecv[s] = total

    for s in range(S):
        for d in range(1, n_chan):
            f_copy(s, d).wait_recv()
    for k in range(P_CAP):
        out[k] = frecv[tab[2 * n + 3 * S + k]].astype(F32) * wt[k]

    for s in range(n):
        for side in range(2):
            y_copy(side, s).wait_send()
    for s in range(S):
        x_copy(s).wait_send()
        for d in range(1, n_z):
            z_copy(s, d).wait_send()
        for d in range(1, n_chan):
            f_copy(s, d).wait_send()


MESH = pl.DeviceIdType.MESH


def pair_facts(pair_blocks, pair_count, blocks_here, n_chan):
    slots = pair_blocks.shape[0]
    rows = jnp.arange(slots, dtype=jnp.int32)
    live = ((rows % P_CAP).reshape(n_chan, P_CAP) < pair_count[:, None]).reshape(slots)
    edge = jnp.where(live, pair_blocks[:, 0] // blocks_here, n_chan)
    same = edge[None, :] == edge[:, None]
    rank = jnp.sum((same & (rows[None, :] < rows[:, None])).astype(jnp.int32), axis=1)
    nodes = jnp.arange(n_chan, dtype=jnp.int32)
    counts = jnp.sum((edge[None, :] == nodes[:, None]).astype(jnp.int32), axis=1)
    return live, edge, rank, counts


def split_edges(counts, n_chan):
    n = jnp.array([t[0] for t in TIERS], jnp.int32)
    S = jnp.array([t[1] for t in TIERS], jnp.int32)
    right = jnp.zeros_like(n)
    fits = jnp.ones_like(n, dtype=bool)
    lefts = []
    for e in range(n_chan):
        left = jnp.minimum(jnp.minimum(n, counts[e]), S - jnp.maximum(right, 1))
        lefts.append(left)
        fits = fits & (jnp.maximum(left, 1) + jnp.maximum(right, 1) <= S)
        right = counts[e] - left
        fits = fits & (right <= n)
    return jnp.stack(lefts, axis=1), fits


def fast_path(tier, lefts, live, edge, rank, traces, pair_blocks):
    n, S = TIERS[tier]
    n_chan = lax.axis_size("chan")
    n_win = lax.axis_size("win")
    n_z = n_win // 2
    p = lax.axis_index("chan")
    _, B, CH, TS = traces.shape
    K = TS + 128
    half = CH // 2
    slots = pair_blocks.shape[0]
    nodes = jnp.arange(n_chan, dtype=jnp.int32)
    lefts = lefts[tier]
    at_edge = edge[:, None] == nodes[None, :]
    left_of = jnp.sum(jnp.where(at_edge, lefts[None, :], 0), axis=1)
    is_left = rank < left_of
    order = jnp.where(is_left, rank, rank - left_of)
    node = jnp.where(is_left, edge, edge + 1)
    left_at_next = jnp.sum(
        jnp.where((edge[:, None] + 1) == nodes[None, :], lefts[None, :], 0), axis=1
    )
    slot = jnp.where(
        order == 0,
        jnp.where(is_left, 0, 1),
        jnp.where(is_left, 1 + order, 1 + jnp.maximum(left_at_next - 1, 0) + order),
    )
    first = pair_blocks[:, 0] % B
    second = pair_blocks[:, 1] % B
    here = jnp.where(is_left, first, second)
    there = jnp.where(is_left, second, first)
    sender = jnp.where(is_left, edge + 1, edge)
    tags = []
    values = []
    t = jnp.arange(n, dtype=jnp.int32)[:, None]
    sends = live[None, :] & (sender == p)[None, :] & (order[None, :] == t)
    tab = [
        jnp.sum(jnp.where(sends & is_left[None, :], there[None, :], 0), axis=1),
        jnp.sum(jnp.where(sends & ~is_left[None, :], there[None, :], 0), axis=1),
    ]
    t = jnp.arange(S, dtype=jnp.int32)[:, None]
    works = live[None, :] & (node == p)[None, :] & (slot[None, :] == t)
    other = jnp.maximum(order - 1, 0) + jnp.where(is_left, 0, n - 1)
    tab += [
        jnp.sum(jnp.where(works, here[None, :], 0), axis=1),
        jnp.sum(jnp.where(works, other[None, :], 0), axis=1),
        jnp.sum(jnp.where(works & is_left[None, :], 1, 0), axis=1),
    ]
    k = jnp.arange(P_CAP, dtype=jnp.int32)[:, None]
    mine = live[None, :] & (jnp.arange(slots, dtype=jnp.int32)[None, :] == p * P_CAP + k)
    source = jnp.mod(p - node, n_chan) * S + slot
    tab.append(jnp.sum(jnp.where(mine, source[None, :], 0), axis=1))
    tab = jnp.concatenate(tab)
    norm_scale = 1.0 / math.sqrt(TS * n_win)
    weights = jnp.sum(jnp.where(mine, norm_scale, 0.0), axis=1).astype(F32)

    dma = pltpu.SemaphoreType.DMA
    result = pl.pallas_call(
        functools.partial(kernel, n, S),
        out_shape=jax.ShapeDtypeStruct((P_CAP, half, 8 * CH), F32),
        in_specs=[
            pl.BlockSpec(memory_space=pltpu.SMEM),
            pl.BlockSpec(memory_space=pltpu.SMEM),
            pl.BlockSpec(memory_space=pl.ANY),
        ],
        out_specs=pl.BlockSpec(memory_space=pltpu.VMEM),
        scratch_shapes=[
            pltpu.VMEM((B, CH, TS), F32),
            pltpu.VMEM((n_z * CH, K), BF16),
            pltpu.VMEM((2, 256, K), BF16),
            pltpu.VMEM((2, n, CH, TS), BF16),
            pltpu.VMEM((2, CH, TS), BF16),
            pltpu.VMEM((2 * (n - 1), CH, TS), BF16),
            pltpu.VMEM((S, n_z, half, 8 * CH), BF16),
            pltpu.VMEM((S, n_z, half, 8 * CH), BF16),
            pltpu.VMEM((n_z, half, 8 * CH), F32),
            pltpu.VMEM((S, n_z, half, 8 * CH), BF16),
            pltpu.VMEM((S, n_z, half, 8 * CH), BF16),
            pltpu.VMEM((S, half, 8 * CH), F32),
            pltpu.VMEM((S, half, 8 * CH), BF16),
            pltpu.VMEM((n_chan * S, half, 8 * CH), BF16),
            dma((B,)),
            dma((2, n)), dma((2, n)),
            dma((S,)), dma((S,)),
            dma((S, n_z)), dma((S, n_z)),
            dma((S, n_chan)), dma((S, n_chan)),
        ],
        compiler_params=pltpu.CompilerParams(collective_id=tier, has_side_effects=True),
        name=f"stack_pairs_{n}_{S}",
    )(tab, weights, traces)
    result = result.reshape(P_CAP, half, 2, 4, CH)
    return jnp.transpose(result, (3, 0, 2, 1, 4)).reshape(4, P_CAP, CH * CH)


def per_device(traces, pair_blocks, pair_count):
    n_chan = lax.axis_size("chan")
    live, edge, rank, counts = pair_facts(pair_blocks, pair_count, traces.shape[1], n_chan)
    lefts, fits = split_edges(counts, n_chan)
    choice = jnp.where(
        fits[0], 0, jnp.where(fits[1], 1, jnp.where(fits[2], 2, 3))
    ).astype(jnp.int32)
    branches = [
        functools.partial(
            lambda tier, t, pb, pc: fast_path(tier, lefts, live, edge, rank, t, pb), tier
        )
        for tier in range(len(TIERS))
    ]
    return lax.switch(choice, branches + [general_path], traces, pair_blocks, pair_count)


def solution(mesh):
    in_specs = (P("win", "chan", None, None), P(), P())
    out_specs = P("win", "chan", None)
    return jax.shard_map(
        per_device, mesh=mesh, in_specs=in_specs, out_specs=out_specs, check_vma=False
    )
```

```python
import functools
import math

import jax
import jax.numpy as jnp
from jax import lax
from jax.experimental import pallas as pl
from jax.experimental.pallas import tpu as pltpu
from jax.sharding import PartitionSpec as P

LAGS = 64
P_CAP = 3
EPS = 1e-06
TIERS = ((2, 4), (3, 4), (4, 6))
BF16 = jnp.bfloat16
F32 = jnp.float32
MESH = pl.DeviceIdType.MESH

N_MAX = max(t[0] for t in TIERS)
S_MAX = max(t[1] for t in TIERS)
HERE = 2 * N_MAX
OTHER = HERE + S_MAX
SIDE = OTHER + S_MAX
SOURCE = SIDE + S_MAX
LIVE = SOURCE + P_CAP
CHOICE = LIVE + P_CAP
TRASH = CHOICE + 1
TAB = TRASH + 1


def whiten(signal):
    centred = signal - jnp.mean(signal, axis=-1, keepdims=True)
    power = jnp.mean(centred * centred, axis=-1, keepdims=True)
    return (centred * lax.rsqrt(power + EPS)).astype(BF16)


def fetch_blocks(traces, requests, per_peer, my_index, blocks_here):
    owners = requests.shape[0]
    home_index = requests // blocks_here
    is_local = home_index == my_index
    slot_rank = jnp.cumsum(is_local.astype(jnp.int32), axis=1) - 1
    chosen = is_local[:, :, None] & (
        slot_rank[:, :, None] == jnp.arange(per_peer, dtype=jnp.int32)[None, None, :]
    )
    local_block = jnp.sum(
        jnp.where(chosen, requests[:, :, None] - my_index * blocks_here, 0), axis=1
    ).reshape(-1)
    is_valid = jnp.any(chosen, axis=1).reshape(1, -1, 1, 1)
    owner_ids = jnp.arange(owners, dtype=jnp.int32)
    my_requests = jnp.sum(jnp.where((owner_ids == my_index)[:, None], requests, 0), axis=0)
    my_home = my_requests // blocks_here
    request_total = my_requests.shape[0]
    request_ids = jnp.arange(request_total, dtype=jnp.int32)
    earlier = request_ids[None, :] < request_ids[:, None]
    my_rank = jnp.sum((earlier & (my_home[None, :] == my_home[:, None])).astype(jnp.int32), axis=1)
    position = my_home * per_peer + my_rank
    outgoing = jnp.where(
        is_valid, jnp.take(traces, local_block, axis=1), jnp.zeros((), jnp.float32)
    )
    incoming = lax.all_to_all(outgoing, "chan", split_axis=1, concat_axis=1, tiled=True)
    return whiten(jnp.take(incoming, position, axis=1))


def general_path(traces, pair_blocks, pair_count):
    owners = lax.axis_size("chan")
    my_index = lax.axis_index("chan")
    blocks_here = traces.shape[1]
    channels = traces.shape[2]
    samples = traces.shape[3]
    windows = traces.shape[0] * lax.axis_size("win")
    norm_scale = 1.0 / math.sqrt(samples * windows)
    pair_table = pair_blocks.reshape(owners, P_CAP, 2)
    owner_ids = jnp.arange(owners, dtype=jnp.int32)
    mine_row = owner_ids == my_index
    my_count = jnp.sum(jnp.where(mine_row, pair_count, 0))
    requests = jnp.concatenate([pair_table[:, :, 0], pair_table[:, P_CAP - 1 :, 1]], axis=1)
    live_mask = (jnp.arange(P_CAP, dtype=jnp.int32) < my_count).astype(jnp.float32)
    fetched = fetch_blocks(traces, requests, 1, my_index, blocks_here)
    left_side = jnp.stack([fetched[:, row] for row in range(P_CAP)], axis=1)
    right_side = jnp.stack([fetched[:, row + 1] for row in range(P_CAP)], axis=1)
    half_lags = LAGS // 2
    padded = jnp.pad(right_side, ((0, 0), (0, 0), (0, 0), (half_lags, half_lags)))
    weights = live_mask * norm_scale
    width = 8

    def lag_block(first_lag):
        shifted = jnp.stack(
            [
                lax.dynamic_slice_in_dim(padded, first_lag + offset_lag, samples, axis=3)
                for offset_lag in range(width)
            ],
            axis=2,
        )
        product = jnp.einsum(
            "wpit,wpgjt->gpij", left_side, shifted, preferred_element_type=jnp.float32
        )
        return product.reshape(width, P_CAP, channels * channels) * weights[None, :, None]

    firsts = jnp.arange(LAGS // width, dtype=jnp.int32) * width
    partial = lax.map(lag_block, firsts).reshape(
        lax.axis_size("win"), -1, P_CAP, channels * channels
    )
    return jnp.sum(
        lax.all_to_all(partial, "win", split_axis=0, concat_axis=0, tiled=True), axis=0
    )


def kernel(
    n, S, scale, tab, traces, out,
    raw, abuf, bbuf, ysend, yfirst, yrest, xsend, xrecv, acc, zsend, zrecv, own, fsend, frecv,
    load_sem, ys_sem, yr_sem, xs_sem, xr_sem, zs_sem, zr_sem, fs_sem, fr_sem,
):
    n_chan = lax.axis_size("chan")
    n_z = lax.axis_size("win") // 2
    p = lax.axis_index("chan")
    w = lax.axis_index("win")
    z = w // 2
    c = w % 2
    B, CH, TS = raw.shape
    half = CH // 2
    K = abuf.shape[1]

    loads = [pltpu.make_async_copy(traces.at[0, b], raw.at[b], load_sem.at[b]) for b in range(B)]
    for copy in loads:
        copy.start()

    barrier = pltpu.get_barrier_semaphore()
    for d in range(1, n_chan):
        pl.semaphore_signal(
            barrier, inc=1, device_id={"chan": lax.rem(p + d, n_chan)}, device_id_type=MESH
        )
    for d in range(1, n_z):
        pl.semaphore_signal(
            barrier, inc=1, device_id={"win": lax.rem(z + d, n_z) * 2 + c}, device_id_type=MESH
        )
    pl.semaphore_signal(barrier, inc=1, device_id={"win": z * 2 + 1 - c}, device_id_type=MESH)

    bbuf[:, 4 * CH :, :] = jnp.zeros((2, bbuf.shape[1] - 4 * CH, K), BF16)
    for copy in loads:
        copy.wait()

    def y_copy(side, s):
        dst = yfirst.at[side] if s == 0 else yrest.at[side * (n - 1) + s - 1]
        peer = lax.rem(p + (n_chan - 1 if side == 0 else 1), n_chan)
        return pltpu.make_async_remote_copy(
            src_ref=ysend.at[side, s], dst_ref=dst,
            send_sem=ys_sem.at[side, s], recv_sem=yr_sem.at[side, s],
            device_id={"chan": peer}, device_id_type=MESH,
        )

    def first_copy(side):
        return pltpu.make_async_remote_copy(
            src_ref=ysend.at[side, 0], dst_ref=yfirst.at[side],
            send_sem=ys_sem.at[side, 0], recv_sem=yr_sem.at[side, 0],
            device_id={"chan": lax.rem(p + 1, n_chan)}, device_id_type=MESH,
        )

    for s in range(n):
        for side in range(2):
            block = tab[side * N_MAX + s]
            for g in range(0, CH, 16):
                ysend[side, s, g : g + 16, :] = whiten(raw[block, g : g + 16, :])
            if s == 0 and side == 0:
                pl.semaphore_wait(barrier, n_chan - 1 + n_z)
            y_copy(side, s).start()

    zeros = jnp.zeros((16, K - TS), BF16)
    low = lax.broadcasted_iota(jnp.int32, (half, 128), 1) < 64

    def fold(C, write):
        for zz in range(n_z):
            top = C[zz * CH : zz * CH + half, :]
            bottom = C[zz * CH + half : (zz + 1) * CH, :]
            r0 = pltpu.roll(bottom[:, 0:128], 64, 1)
            r1 = pltpu.roll(bottom[:, 128:256], 64, 1)
            write(zz, 0, top[:, 0:128])
            write(zz, 1, jnp.where(low, top[:, 128:256], r0))
            write(zz, 2, jnp.where(low, r0, r1))

    def dot(index):
        return lax.dot_general(
            abuf[...], bbuf[index], (((1,), (1,)), ((), ())), preferred_element_type=F32
        )

    def x_copy(s):
        return pltpu.make_async_remote_copy(
            src_ref=xsend.at[s], dst_ref=xrecv.at[s],
            send_sem=xs_sem.at[s], recv_sem=xr_sem.at[s],
            device_id={"win": z * 2 + 1 - c}, device_id_type=MESH,
        )

    def z_copy(s, d):
        peer = lax.rem(z + d, n_z)
        return pltpu.make_async_remote_copy(
            src_ref=zsend.at[s, peer], dst_ref=zrecv.at[s, d],
            send_sem=zs_sem.at[s, d], recv_sem=zr_sem.at[s, d],
            device_id={"win": peer * 2 + c}, device_id_type=MESH,
        )

    def f_copy(s, d):
        return pltpu.make_async_remote_copy(
            src_ref=fsend.at[s], dst_ref=frecv.at[d * S + s],
            send_sem=fs_sem.at[s, d], recv_sem=fr_sem.at[s, d],
            device_id={"chan": lax.rem(p + d, n_chan)}, device_id_type=MESH,
        )

    def correlate(s, other_of):
        block = tab[HERE + s]
        for g in range(0, CH, 16):
            mine = whiten(raw[block, g : g + 16, :])
            other, is_left = other_of(g)
            left = jnp.where(is_left, mine, other)
            right = jnp.where(is_left, other, mine)
            left = jnp.concatenate([left, zeros], axis=1)
            right = jnp.concatenate([right, zeros], axis=1)
            for zz in range(n_z):
                row = zz * CH + g
                abuf[row : row + 16, :] = pltpu.roll(left, (8 * zz - 25) % K, 1)
            for u in range(8):
                row = (u % 4) * CH + g
                bbuf[u // 4, row : row + 16, :] = pltpu.roll(right, 7 - u, 1)

        def write_send(zz, t, value):
            xsend[s, zz, :, t * 128 : (t + 1) * 128] = value.astype(BF16)

        def write_acc(zz, t, value):
            acc[zz, :, t * 128 : (t + 1) * 128] = value

        fold(dot(1 - c), write_send)
        x_copy(s).start()
        fold(dot(c), write_acc)
        x_copy(s).wait_recv()
        for zz in range(n_z):
            zsend[s, zz] = (acc[zz] + xrecv[s, zz].astype(F32)).astype(BF16)
        own[s] = acc[z] + xrecv[s, z].astype(F32)
        for d in range(1, n_z):
            z_copy(s, d).start()

    @pl.loop(0, 2)
    def _(s):
        first_copy(s).wait_recv()
        correlate(s, lambda g: (yfirst[s, g : g + 16, :], s == 0))

    for side in range(2):
        for t in range(1, n):
            y_copy(side, t).wait_recv()

    @pl.loop(2, S)
    def _(s):
        correlate(s, lambda g: (yrest[tab[OTHER + s], g : g + 16, :], tab[SIDE + s] == 1))

    for s in range(S):
        total = own[s]
        for d in range(1, n_z):
            z_copy(s, d).wait_recv()
            total = total + zrecv[s, d].astype(F32)
        total = total.astype(BF16)
        fsend[s] = total
        for d in range(1, n_chan):
            f_copy(s, d).start()
        frecv[s] = total

    for s in range(S):
        for d in range(1, n_chan):
            f_copy(s, d).wait_recv()
    for k in range(P_CAP):
        out[k] = frecv[tab[SOURCE + k]].astype(F32) * (tab[LIVE + k].astype(F32) * scale)

    for s in range(n):
        for side in range(2):
            y_copy(side, s).wait_send()
    for s in range(S):
        x_copy(s).wait_send()
        for d in range(1, n_z):
            z_copy(s, d).wait_send()
        for d in range(1, n_chan):
            f_copy(s, d).wait_send()


def table_kernel(B, n_chan, blocks, pair_count, tab, counts, ranks, lefts):
    p = lax.axis_index("chan")
    for e in range(n_chan + 4):
        counts[e] = 0
        ranks[e] = 0
        lefts[e] = 0
    for t in range(TAB):
        tab[t] = 0
    starts = []
    lives = []
    for o in range(n_chan):
        start = blocks[2 * P_CAP * o] // B
        live = pair_count[o]
        starts.append(start)
        lives.append(live)
        for k in range(P_CAP):
            counts[start + k] = counts[start + k] + (k < live).astype(jnp.int32)
    rights = [0] * len(TIERS)
    fits = [True] * len(TIERS)
    split = [[] for _ in TIERS]
    for e in range(n_chan):
        count = counts[e]
        for t, (n, S) in enumerate(TIERS):
            right = jnp.maximum(rights[t], 1)
            left = jnp.minimum(jnp.minimum(n, count), S - right)
            split[t].append(left)
            fit = jnp.logical_and(jnp.maximum(left, 1) + right <= S, count - left <= n)
            fits[t] = jnp.logical_and(fits[t], fit)
            rights[t] = count - left
    choice = jnp.int32(len(TIERS))
    n, S = jnp.int32(TIERS[-1][0]), jnp.int32(TIERS[-1][1])
    for t in reversed(range(len(TIERS))):
        choice = jnp.where(fits[t], t, choice)
        n = jnp.where(fits[t], TIERS[t][0], n)
        S = jnp.where(fits[t], TIERS[t][1], S)
    for e in range(n_chan):
        left = split[-1][e]
        for t in reversed(range(len(TIERS))):
            left = jnp.where(fits[t], split[t][e], left)
        lefts[e + 1] = left
    tab[CHOICE] = choice
    for o in range(n_chan):
        for k in range(P_CAP):
            edge = starts[o] + k
            live = k < lives[o]
            rank = ranks[edge]
            ranks[edge] = rank + live.astype(jnp.int32)
            left_here = lefts[edge + 1]
            is_left = rank < left_here
            order = jnp.where(is_left, rank, rank - left_here)
            node = jnp.where(is_left, edge, edge + 1)
            rest = jnp.where(is_left, 1, jnp.maximum(lefts[edge + 2], 1)) + order
            slot = jnp.where(order == 0, jnp.where(is_left, 0, 1), rest)
            first = blocks[2 * (P_CAP * o + k)] - edge * B
            second = blocks[2 * (P_CAP * o + k) + 1] - (edge + 1) * B
            here = jnp.where(is_left, first, second)
            there = jnp.where(is_left, second, first)
            sends = jnp.logical_and(live, 2 * edge + 1 - node == p)
            tab[jnp.where(sends, jnp.where(is_left, 0, N_MAX) + order, TRASH)] = there
            works = jnp.logical_and(live, node == p)
            other = jnp.maximum(order - 1, 0) + jnp.where(is_left, 0, n - 1)
            tab[jnp.where(works, HERE + slot, TRASH)] = here
            tab[jnp.where(works, OTHER + slot, TRASH)] = other
            tab[jnp.where(works, SIDE + slot, TRASH)] = is_left.astype(jnp.int32)
            mine = jnp.logical_and(live, p == o)
            away = p - node
            away = jnp.where(away < 0, away + n_chan, away)
            tab[jnp.where(mine, SOURCE + k, TRASH)] = away * S + slot
            tab[jnp.where(mine, LIVE + k, TRASH)] = 1


def fast_path(tier, traces, tab):
    n, S = TIERS[tier]
    n_chan = lax.axis_size("chan")
    n_win = lax.axis_size("win")
    n_z = n_win // 2
    _, B, CH, TS = traces.shape
    K = TS + 128
    half = CH // 2

    dma = pltpu.SemaphoreType.DMA
    result = pl.pallas_call(
        functools.partial(kernel, n, S, 1.0 / math.sqrt(TS * n_win)),
        out_shape=jax.ShapeDtypeStruct((P_CAP, half, 8 * CH), F32),
        in_specs=[
            pl.BlockSpec(memory_space=pltpu.SMEM),
            pl.BlockSpec(memory_space=pl.ANY),
        ],
        out_specs=pl.BlockSpec(memory_space=pltpu.VMEM),
        scratch_shapes=[
            pltpu.VMEM((B, CH, TS), F32),
            pltpu.VMEM((n_z * CH, K), BF16),
            pltpu.VMEM((2, 256, K), BF16),
            pltpu.VMEM((2, n, CH, TS), BF16),
            pltpu.VMEM((2, CH, TS), BF16),
            pltpu.VMEM((2 * (n - 1), CH, TS), BF16),
            pltpu.VMEM((S, n_z, half, 8 * CH), BF16),
            pltpu.VMEM((S, n_z, half, 8 * CH), BF16),
            pltpu.VMEM((n_z, half, 8 * CH), F32),
            pltpu.VMEM((S, n_z, half, 8 * CH), BF16),
            pltpu.VMEM((S, n_z, half, 8 * CH), BF16),
            pltpu.VMEM((S, half, 8 * CH), F32),
            pltpu.VMEM((S, half, 8 * CH), BF16),
            pltpu.VMEM((n_chan * S, half, 8 * CH), BF16),
            dma((B,)),
            dma((2, n)), dma((2, n)),
            dma((S,)), dma((S,)),
            dma((S, n_z)), dma((S, n_z)),
            dma((S, n_chan)), dma((S, n_chan)),
        ],
        compiler_params=pltpu.CompilerParams(collective_id=tier, has_side_effects=True),
        name=f"stack_pairs_{n}_{S}",
    )(tab, traces)
    result = result.reshape(P_CAP, half, 2, 4, CH)
    return jnp.transpose(result, (3, 0, 2, 1, 4)).reshape(4, P_CAP, CH * CH)


def per_device(traces, pair_blocks, pair_count):
    n_chan = lax.axis_size("chan")
    smem = pl.BlockSpec(memory_space=pltpu.SMEM)
    tab = pl.pallas_call(
        functools.partial(table_kernel, traces.shape[1], n_chan),
        out_shape=jax.ShapeDtypeStruct((TAB,), jnp.int32),
        in_specs=[smem, smem],
        out_specs=smem,
        scratch_shapes=[pltpu.SMEM((n_chan + 4,), jnp.int32)] * 3,
        name="pair_tables",
    )(pair_blocks.reshape(-1), pair_count)
    branches = [
        functools.partial(lambda tier, t, tab, pb, pc: fast_path(tier, t, tab), tier)
        for tier in range(len(TIERS))
    ]
    branches.append(lambda t, tab, pb, pc: general_path(t, pb, pc))
    return lax.switch(tab[CHOICE], branches, traces, tab, pair_blocks, pair_count)


def solution(mesh):
    in_specs = (P("win", "chan", None, None), P(), P())
    out_specs = P("win", "chan", None)
    return jax.shard_map(
        per_device, mesh=mesh, in_specs=in_specs, out_specs=out_specs, check_vma=False
    )
```

```python
import functools
import math

import jax
import jax.numpy as jnp
from jax import lax
from jax.experimental import pallas as pl
from jax.experimental.pallas import tpu as pltpu
from jax.sharding import PartitionSpec as P

LAGS = 64
P_CAP = 3
EPS = 1e-06
TIERS = ((2, 4), (3, 4), (4, 6))
FINISH = {4: ((3, 0),), 6: ((3, 0), (4, 1), (5, 2))}
BF16 = jnp.bfloat16
F32 = jnp.float32
MESH = pl.DeviceIdType.MESH

N_MAX = max(t[0] for t in TIERS)
S_MAX = max(t[1] for t in TIERS)
HERE = 2 * N_MAX
OTHER = HERE + S_MAX
SOURCE = OTHER + S_MAX
LIVE = SOURCE + P_CAP
TRASH = LIVE + P_CAP
TAB = TRASH + 1


def whiten(signal):
    centred = signal - jnp.mean(signal, axis=-1, keepdims=True)
    power = jnp.mean(centred * centred, axis=-1, keepdims=True)
    return (centred * lax.rsqrt(power + EPS)).astype(BF16)


def fetch_blocks(traces, requests, per_peer, my_index, blocks_here):
    owners = requests.shape[0]
    home_index = requests // blocks_here
    is_local = home_index == my_index
    slot_rank = jnp.cumsum(is_local.astype(jnp.int32), axis=1) - 1
    chosen = is_local[:, :, None] & (
        slot_rank[:, :, None] == jnp.arange(per_peer, dtype=jnp.int32)[None, None, :]
    )
    local_block = jnp.sum(
        jnp.where(chosen, requests[:, :, None] - my_index * blocks_here, 0), axis=1
    ).reshape(-1)
    is_valid = jnp.any(chosen, axis=1).reshape(1, -1, 1, 1)
    owner_ids = jnp.arange(owners, dtype=jnp.int32)
    my_requests = jnp.sum(jnp.where((owner_ids == my_index)[:, None], requests, 0), axis=0)
    my_home = my_requests // blocks_here
    request_total = my_requests.shape[0]
    request_ids = jnp.arange(request_total, dtype=jnp.int32)
    earlier = request_ids[None, :] < request_ids[:, None]
    my_rank = jnp.sum((earlier & (my_home[None, :] == my_home[:, None])).astype(jnp.int32), axis=1)
    position = my_home * per_peer + my_rank
    outgoing = jnp.where(
        is_valid, jnp.take(traces, local_block, axis=1), jnp.zeros((), jnp.float32)
    )
    incoming = lax.all_to_all(outgoing, "chan", split_axis=1, concat_axis=1, tiled=True)
    return whiten(jnp.take(incoming, position, axis=1))


def general_path(traces, pair_blocks, pair_count):
    owners = lax.axis_size("chan")
    my_index = lax.axis_index("chan")
    blocks_here = traces.shape[1]
    channels = traces.shape[2]
    samples = traces.shape[3]
    windows = traces.shape[0] * lax.axis_size("win")
    norm_scale = 1.0 / math.sqrt(samples * windows)
    pair_table = pair_blocks.reshape(owners, P_CAP, 2)
    owner_ids = jnp.arange(owners, dtype=jnp.int32)
    mine_row = owner_ids == my_index
    my_count = jnp.sum(jnp.where(mine_row, pair_count, 0))
    requests = jnp.concatenate([pair_table[:, :, 0], pair_table[:, P_CAP - 1 :, 1]], axis=1)
    live_mask = (jnp.arange(P_CAP, dtype=jnp.int32) < my_count).astype(jnp.float32)
    fetched = fetch_blocks(traces, requests, 1, my_index, blocks_here)
    left_side = jnp.stack([fetched[:, row] for row in range(P_CAP)], axis=1)
    right_side = jnp.stack([fetched[:, row + 1] for row in range(P_CAP)], axis=1)
    half_lags = LAGS // 2
    padded = jnp.pad(right_side, ((0, 0), (0, 0), (0, 0), (half_lags, half_lags)))
    weights = live_mask * norm_scale
    width = 8

    def lag_block(first_lag):
        shifted = jnp.stack(
            [
                lax.dynamic_slice_in_dim(padded, first_lag + offset_lag, samples, axis=3)
                for offset_lag in range(width)
            ],
            axis=2,
        )
        product = jnp.einsum(
            "wpit,wpgjt->gpij", left_side, shifted, preferred_element_type=jnp.float32
        )
        return product.reshape(width, P_CAP, channels * channels) * weights[None, :, None]

    firsts = jnp.arange(LAGS // width, dtype=jnp.int32) * width
    partial = lax.map(lag_block, firsts).reshape(
        lax.axis_size("win"), -1, P_CAP, channels * channels
    )
    return jnp.sum(
        lax.all_to_all(partial, "win", split_axis=0, concat_axis=0, tiled=True), axis=0
    )


def kernel(
    n, S, scale, tab, traces, out,
    raw, abuf, bbuf, ysend, mine, other, xsend, xrecv, acc, zsend, zrecv, own, fsend, frecv,
    load_sem, ys_sem, yr_sem, xs_sem, xr_sem, zs_sem, zr_sem, fs_sem, fr_sem, z_in, chan_in,
    *yrecv,
):
    n_chan = lax.axis_size("chan")
    n_z = lax.axis_size("win") // 2
    p = lax.axis_index("chan")
    w = lax.axis_index("win")
    z = w // 2
    c = w % 2
    B, CH, TS = raw.shape
    half = CH // 2
    K = abuf.shape[1]

    loads = [pltpu.make_async_copy(traces.at[0, b], raw.at[b], load_sem.at[b]) for b in range(B)]
    for copy in loads:
        copy.start()

    barrier = pltpu.get_barrier_semaphore()
    def chan_peer(d):
        return {"chan": lax.rem(p + d + n_chan, n_chan)}

    def z_peer(d):
        return {"win": lax.rem(z + d + n_z, n_z) * 2 + c}

    def signal(sem, device):
        pl.semaphore_signal(sem, inc=1, device_id=device, device_id_type=MESH)

    for d in (-1, 1):
        signal(barrier, chan_peer(d))
        signal(barrier, z_peer(d))
    signal(barrier, {"win": z * 2 + 1 - c})

    bbuf[:, 4 * CH :, :] = jnp.zeros((2, bbuf.shape[1] - 4 * CH, K), BF16)
    for copy in loads:
        copy.wait()

    def y_copy(side, s):
        dst = yrecv[s].at[side]
        peer = lax.rem(p + (n_chan - 1 if side == 0 else 1), n_chan)
        return pltpu.make_async_remote_copy(
            src_ref=ysend.at[side, s], dst_ref=dst,
            send_sem=ys_sem.at[side, s], recv_sem=yr_sem.at[side, s],
            device_id={"chan": peer}, device_id_type=MESH,
        )

    for s in range(n):
        for side in range(2):
            block = tab[side * N_MAX + s]
            for g in range(0, CH, 16):
                ysend[side, s, g : g + 16, :] = whiten(raw[block, g : g + 16, :])
            if s == 0 and side == 0:
                pl.semaphore_wait(barrier, 5)
            y_copy(side, s).start()
            if s == 0 and side == 1:
                for d in (-1, 1):
                    signal(z_in.at[0], z_peer(d))
                    signal(chan_in.at[0], chan_peer(d))
            if s == n - 1 and side == 1:
                pl.semaphore_wait(z_in.at[0], 2)
                pl.semaphore_wait(chan_in.at[0], 2)
                for d in (-2, 2):
                    signal(z_in.at[1], z_peer(d))
                    signal(chan_in.at[1], chan_peer(d))

    for s in range(S):
        block = tab[HERE + s]
        for g in range(0, CH, 16):
            mine[s, g : g + 16, :] = whiten(raw[block, g : g + 16, :])

    zeros = jnp.zeros((16, K - TS), BF16)
    low = lax.broadcasted_iota(jnp.int32, (half, 128), 1) < 64

    def fold(C, write):
        for zz in range(n_z):
            top = C[zz * CH : zz * CH + half, :]
            bottom = C[zz * CH + half : (zz + 1) * CH, :]
            r0 = pltpu.roll(bottom[:, 0:128], 64, 1)
            r1 = pltpu.roll(bottom[:, 128:256], 64, 1)
            write(zz, 0, top[:, 0:128])
            write(zz, 1, jnp.where(low, top[:, 128:256], r0))
            write(zz, 2, jnp.where(low, r0, r1))

    def dot(index):
        return lax.dot_general(
            abuf[...], bbuf[index], (((1,), (1,)), ((), ())), preferred_element_type=F32
        )

    def x_copy(s):
        return pltpu.make_async_remote_copy(
            src_ref=xsend.at[s], dst_ref=xrecv.at[s],
            send_sem=xs_sem.at[s], recv_sem=xr_sem.at[s],
            device_id={"win": z * 2 + 1 - c}, device_id_type=MESH,
        )

    def z_copy(s, d):
        peer = lax.rem(z + d, n_z)
        return pltpu.make_async_remote_copy(
            src_ref=zsend.at[s, peer], dst_ref=zrecv.at[s, d],
            send_sem=zs_sem.at[s, d], recv_sem=zr_sem.at[s, d],
            device_id={"win": peer * 2 + c}, device_id_type=MESH,
        )

    def f_copy(s, d):
        return pltpu.make_async_remote_copy(
            src_ref=fsend.at[s], dst_ref=frecv.at[d * S + s],
            send_sem=fs_sem.at[s, d], recv_sem=fr_sem.at[s, d],
            device_id={"chan": lax.rem(p + d, n_chan)}, device_id_type=MESH,
        )

    def finish(s):
        if s == 0:
            pl.semaphore_wait(chan_in.at[2], 2)
        total = own[s]
        for d in range(1, n_z):
            z_copy(s, d).wait_recv()
            total = total + zrecv[s, d].astype(F32)
        total = total.astype(BF16)
        fsend[s] = total
        for d in range(1, n_chan):
            f_copy(s, d).start()
        frecv[s] = total

    @pl.loop(0, S)
    def _(s):
        for side in range(2):

            @pl.when(s == side)
            def _():
                y_copy(side, 0).wait_recv()
                other[...] = yrecv[0][side]

        for t in range(1, n):

            @pl.when(s == t + 1)
            def _():
                for side in range(2):
                    y_copy(side, t).wait_recv()

            @pl.when(s == t + 1 if t < n - 1 else s > t)
            def _():
                order = tab[OTHER + s] // 2
                side = 1 - tab[OTHER + s] % 2
                for g in range(0, CH, 16):
                    value = yrecv[1][side, g : g + 16, :]
                    for u in range(2, t + 1):
                        value = jnp.where(order == u, yrecv[u][side, g : g + 16, :], value)
                    other[g : g + 16, :] = value

        for late, early in FINISH[S]:

            @pl.when(s == late)
            def _():
                finish(early)

        is_left = jnp.where(s < 2, 1 - s, tab[OTHER + s] % 2) == 1
        for g in range(0, CH, 16):
            ours = mine[s, g : g + 16, :]
            theirs = other[g : g + 16, :]
            left = jnp.where(is_left, ours, theirs)
            right = jnp.where(is_left, theirs, ours)
            left = jnp.concatenate([left, zeros], axis=1)
            right = jnp.concatenate([right, zeros], axis=1)
            for zz in range(n_z):
                row = zz * CH + g
                abuf[row : row + 16, :] = pltpu.roll(left, (8 * zz - 25) % K, 1)
            for u in range(8):
                row = (u % 4) * CH + g
                bbuf[u // 4, row : row + 16, :] = pltpu.roll(right, 7 - u, 1)

        def write_send(zz, t, value):
            xsend[s, zz, :, t * 128 : (t + 1) * 128] = value.astype(BF16)

        def write_acc(zz, t, value):
            acc[zz, :, t * 128 : (t + 1) * 128] = value

        fold(dot(1 - c), write_send)
        x_copy(s).start()
        fold(dot(c), write_acc)
        x_copy(s).wait_recv()
        for zz in range(n_z):
            zsend[s, zz] = (acc[zz] + xrecv[s, zz].astype(F32)).astype(BF16)
        own[s] = acc[z] + xrecv[s, z].astype(F32)

        @pl.when(s == 0)
        def _():
            pl.semaphore_wait(z_in.at[1], 2)
            pl.semaphore_wait(chan_in.at[1], 2)
            for d in (-4, 4):
                signal(chan_in.at[2], chan_peer(d))

        for d in range(1, n_z):
            z_copy(s, d).start()

    done = [early for _, early in FINISH[S]]
    for s in range(S):
        if s not in done:
            finish(s)

    for s in range(n):
        for side in range(2):
            y_copy(side, s).wait_send()
    for s in range(S):
        x_copy(s).wait_send()
        for d in range(1, n_z):
            z_copy(s, d).wait_send()
        for d in range(1, n_chan):
            f_copy(s, d).wait_send()
    for s in range(S):
        for d in range(1, n_chan):
            f_copy(s, d).wait_recv()
    for k in range(P_CAP):
        out[k] = frecv[tab[SOURCE + k]].astype(F32) * (tab[LIVE + k].astype(F32) * scale)


def table_kernel(B, n_chan, blocks, pair_count, tab, tier, counts, lefts):
    p = lax.axis_index("chan")
    for e in range(n_chan + 4):
        counts[e] = 0
        lefts[e] = 0
    for t in range(TAB):
        tab[t] = 0
    starts = [blocks[0, P_CAP * o] // B for o in range(n_chan)]
    lives = [pair_count[o] for o in range(n_chan)]
    for start, live in zip(starts, lives):
        counts[start] = counts[start] + 1
        counts[start + live] = counts[start + live] - 1
    rights = [0] * len(TIERS)
    fits = [True] * len(TIERS)
    split = [[] for _ in TIERS]
    count = 0
    for e in range(n_chan):
        count = count + counts[e]
        for t, (n, S) in enumerate(TIERS):
            right = jnp.maximum(rights[t], 1)
            left = jnp.minimum(jnp.minimum(n, count), S - right)
            split[t].append(left)
            fit = jnp.logical_and(jnp.maximum(left, 1) + right <= S, count - left <= n)
            fits[t] = jnp.logical_and(fits[t], fit)
            rights[t] = count - left
    choice = jnp.int32(len(TIERS))
    S = jnp.int32(TIERS[-1][1])
    for t in reversed(range(len(TIERS))):
        choice = jnp.where(fits[t], t, choice)
        S = jnp.where(fits[t], TIERS[t][1], S)
    for e in range(n_chan):
        left = split[-1][e]
        for t in reversed(range(len(TIERS))):
            left = jnp.where(fits[t], split[t][e], left)
        lefts[e + 1] = left
    tier[0] = choice

    ranks = [0, 0]
    left_of = [lefts[p], lefts[p + 1]]
    rest_of_right = jnp.maximum(left_of[1], 1)
    for o, (start, live) in enumerate(zip(starts, lives)):
        for end in range(2):
            k = p - 1 + end - start
            here = jnp.logical_and(k >= 0, k < live)
            row = P_CAP * o + jnp.minimum(jnp.maximum(k, 0), P_CAP - 1)
            block = blocks[1 - end, row] - p * B
            rank = ranks[end]
            ranks[end] = rank + here.astype(jnp.int32)
            is_left = rank < left_of[end]
            order = jnp.where(is_left, rank, rank - left_of[end])
            if end == 0:
                works = jnp.logical_not(is_left)
                slot = jnp.where(order == 0, 1, rest_of_right + order)
            else:
                works = is_left
                slot = jnp.where(order == 0, 0, 1 + order)
            place = jnp.where(works, HERE + slot, end * N_MAX + order)
            tab[jnp.where(here, place, TRASH)] = block
            tab[jnp.where(jnp.logical_and(here, works), OTHER + slot, TRASH)] = 2 * order + end

    own_start = blocks[0, P_CAP * p] // B
    own_live = pair_count[p]
    for k in range(P_CAP):
        edge = own_start + k
        rank = 0
        for o, (start, live) in enumerate(zip(starts, lives)):
            inside = jnp.logical_and(edge >= start, edge < start + live)
            rank = rank + jnp.logical_and(inside, o < p).astype(jnp.int32)
        left = lefts[edge + 1]
        is_left = rank < left
        order = jnp.where(is_left, rank, rank - left)
        rest = jnp.where(is_left, 1, jnp.maximum(lefts[edge + 2], 1)) + order
        slot = jnp.where(order == 0, jnp.where(is_left, 0, 1), rest)
        away = p - jnp.where(is_left, edge, edge + 1)
        away = jnp.where(away < 0, away + n_chan, away)
        live = k < own_live
        tab[SOURCE + k] = jnp.where(live, away * S + slot, 0)
        tab[LIVE + k] = live.astype(jnp.int32)


def fast_path(tier, traces, tab):
    n, S = TIERS[tier]
    n_chan = lax.axis_size("chan")
    n_win = lax.axis_size("win")
    n_z = n_win // 2
    _, B, CH, TS = traces.shape
    K = TS + 128
    half = CH // 2

    dma = pltpu.SemaphoreType.DMA
    result = pl.pallas_call(
        functools.partial(kernel, n, S, 1.0 / math.sqrt(TS * n_win)),
        out_shape=jax.ShapeDtypeStruct((P_CAP, half, 8 * CH), F32),
        in_specs=[
            pl.BlockSpec(memory_space=pltpu.SMEM),
            pl.BlockSpec(memory_space=pl.ANY),
        ],
        out_specs=pl.BlockSpec(memory_space=pltpu.VMEM),
        scratch_shapes=[
            pltpu.VMEM((B, CH, TS), F32),
            pltpu.VMEM((n_z * CH, K), BF16),
            pltpu.VMEM((2, 256, K), BF16),
            pltpu.VMEM((2, n, CH, TS), BF16),
            pltpu.VMEM((S, CH, TS), BF16),
            pltpu.VMEM((CH, TS), BF16),
            pltpu.VMEM((S, n_z, half, 8 * CH), BF16),
            pltpu.VMEM((S, n_z, half, 8 * CH), BF16),
            pltpu.VMEM((n_z, half, 8 * CH), F32),
            pltpu.VMEM((S, n_z, half, 8 * CH), BF16),
            pltpu.VMEM((S, n_z, half, 8 * CH), BF16),
            pltpu.VMEM((S, half, 8 * CH), F32),
            pltpu.VMEM((S, half, 8 * CH), BF16),
            pltpu.VMEM((n_chan * S, half, 8 * CH), BF16),
            dma((B,)),
            dma((2, n)), dma((2, n)),
            dma((S,)), dma((S,)),
            dma((S, n_z)), dma((S, n_z)),
            dma((S, n_chan)), dma((S, n_chan)),
            pltpu.SemaphoreType.REGULAR((2,)), pltpu.SemaphoreType.REGULAR((3,)),
        ]
        + [pltpu.VMEM((2, CH, TS), BF16)] * n,
        compiler_params=pltpu.CompilerParams(collective_id=tier, has_side_effects=True),
        name=f"stack_pairs_{n}_{S}",
    )(tab, traces)
    result = result.reshape(P_CAP, half, 2, 4, CH)
    return jnp.transpose(result, (3, 0, 2, 1, 4)).reshape(4, P_CAP, CH * CH)


def per_device(traces, pair_blocks, pair_count):
    n_chan = lax.axis_size("chan")
    smem = pl.BlockSpec(memory_space=pltpu.SMEM)
    tab, tier = pl.pallas_call(
        functools.partial(table_kernel, traces.shape[1], n_chan),
        out_shape=(jax.ShapeDtypeStruct((TAB,), jnp.int32), jax.ShapeDtypeStruct((1,), jnp.int32)),
        in_specs=[smem, smem],
        out_specs=(smem, smem),
        scratch_shapes=[pltpu.SMEM((n_chan + 4,), jnp.int32)] * 2,
        name="pair_tables",
    )(pair_blocks.T, pair_count)
    branches = [
        functools.partial(lambda tier, t, tab, pb, pc: fast_path(tier, t, tab), tier)
        for tier in range(len(TIERS))
    ]
    branches.append(lambda t, tab, pb, pc: general_path(t, pb, pc))
    return lax.switch(tier.reshape(()), branches, traces, tab, pair_blocks, pair_count)


def solution(mesh):
    in_specs = (P("win", "chan", None, None), P(), P())
    out_specs = P("win", "chan", None)
    return jax.shard_map(
        per_device, mesh=mesh, in_specs=in_specs, out_specs=out_specs, check_vma=False
    )
```

```python
import functools
import math

import jax
import jax.numpy as jnp
from jax import lax
from jax.experimental import pallas as pl
from jax.experimental.pallas import tpu as pltpu
from jax.sharding import PartitionSpec as P

LAGS = 64
P_CAP = 3
EPS = 1e-06
TIERS = ((2, 3), (3, 4), (4, 5), (4, 6))
DIRECT = (4, 3, 5, 2, 6, 1, 7)
FINISH = {3: (), 4: (), 5: ((4, 0),), 6: ((4, 0), (5, 1))}
BF16 = jnp.bfloat16
F32 = jnp.float32
MESH = pl.DeviceIdType.MESH

N_MAX = max(t[0] for t in TIERS)
S_MAX = max(t[1] for t in TIERS)
HERE = 2 * N_MAX
OTHER = HERE + S_MAX
SOURCE = OTHER + S_MAX
LIVE = SOURCE + P_CAP
TRASH = LIVE + P_CAP
TAB = TRASH + 1


def whiten(signal):
    centred = signal - jnp.mean(signal, axis=-1, keepdims=True)
    power = jnp.mean(centred * centred, axis=-1, keepdims=True)
    return (centred * lax.rsqrt(power + EPS)).astype(BF16)


def fetch_blocks(traces, requests, per_peer, my_index, blocks_here):
    owners = requests.shape[0]
    home_index = requests // blocks_here
    is_local = home_index == my_index
    slot_rank = jnp.cumsum(is_local.astype(jnp.int32), axis=1) - 1
    chosen = is_local[:, :, None] & (
        slot_rank[:, :, None] == jnp.arange(per_peer, dtype=jnp.int32)[None, None, :]
    )
    local_block = jnp.sum(
        jnp.where(chosen, requests[:, :, None] - my_index * blocks_here, 0), axis=1
    ).reshape(-1)
    is_valid = jnp.any(chosen, axis=1).reshape(1, -1, 1, 1)
    owner_ids = jnp.arange(owners, dtype=jnp.int32)
    my_requests = jnp.sum(jnp.where((owner_ids == my_index)[:, None], requests, 0), axis=0)
    my_home = my_requests // blocks_here
    request_total = my_requests.shape[0]
    request_ids = jnp.arange(request_total, dtype=jnp.int32)
    earlier = request_ids[None, :] < request_ids[:, None]
    my_rank = jnp.sum((earlier & (my_home[None, :] == my_home[:, None])).astype(jnp.int32), axis=1)
    position = my_home * per_peer + my_rank
    outgoing = jnp.where(
        is_valid, jnp.take(traces, local_block, axis=1), jnp.zeros((), jnp.float32)
    )
    incoming = lax.all_to_all(outgoing, "chan", split_axis=1, concat_axis=1, tiled=True)
    return whiten(jnp.take(incoming, position, axis=1))


def general_path(traces, pair_blocks, pair_count):
    owners = lax.axis_size("chan")
    my_index = lax.axis_index("chan")
    blocks_here = traces.shape[1]
    channels = traces.shape[2]
    samples = traces.shape[3]
    windows = traces.shape[0] * lax.axis_size("win")
    norm_scale = 1.0 / math.sqrt(samples * windows)
    pair_table = pair_blocks.reshape(owners, P_CAP, 2)
    owner_ids = jnp.arange(owners, dtype=jnp.int32)
    mine_row = owner_ids == my_index
    my_count = jnp.sum(jnp.where(mine_row, pair_count, 0))
    requests = jnp.concatenate([pair_table[:, :, 0], pair_table[:, P_CAP - 1 :, 1]], axis=1)
    live_mask = (jnp.arange(P_CAP, dtype=jnp.int32) < my_count).astype(jnp.float32)
    fetched = fetch_blocks(traces, requests, 1, my_index, blocks_here)
    left_side = jnp.stack([fetched[:, row] for row in range(P_CAP)], axis=1)
    right_side = jnp.stack([fetched[:, row + 1] for row in range(P_CAP)], axis=1)
    half_lags = LAGS // 2
    padded = jnp.pad(right_side, ((0, 0), (0, 0), (0, 0), (half_lags, half_lags)))
    weights = live_mask * norm_scale
    width = 8

    def lag_block(first_lag):
        shifted = jnp.stack(
            [
                lax.dynamic_slice_in_dim(padded, first_lag + offset_lag, samples, axis=3)
                for offset_lag in range(width)
            ],
            axis=2,
        )
        product = jnp.einsum(
            "wpit,wpgjt->gpij", left_side, shifted, preferred_element_type=jnp.float32
        )
        return product.reshape(width, P_CAP, channels * channels) * weights[None, :, None]

    firsts = jnp.arange(LAGS // width, dtype=jnp.int32) * width
    partial = lax.map(lag_block, firsts).reshape(
        lax.axis_size("win"), -1, P_CAP, channels * channels
    )
    return jnp.sum(
        lax.all_to_all(partial, "win", split_axis=0, concat_axis=0, tiled=True), axis=0
    )


def kernel(
    n, S, scale, tab, traces, out,
    raw, abuf, bbuf, ysend, mine, other, xsend, xrecv, acc, zsend, zrecv, own, fsend, frecv,
    load_sem, ys_sem, yr_sem, xs_sem, xr_sem, zs_sem, zr_sem, fs_sem, fr_sem, z_in, chan_in,
    *yrecv,
):
    n_chan = lax.axis_size("chan")
    n_z = lax.axis_size("win") // 2
    p = lax.axis_index("chan")
    w = lax.axis_index("win")
    z = w // 2
    c = w % 2
    B, CH, TS = raw.shape
    half = CH // 2
    K = abuf.shape[1]

    barrier = pltpu.get_barrier_semaphore()
    def chan_peer(d):
        return {"chan": lax.rem(p + d + n_chan, n_chan)}

    def z_peer(d):
        return {"win": lax.rem(z + d + n_z, n_z) * 2 + c}

    def signal(sem, device):
        pl.semaphore_signal(sem, inc=1, device_id=device, device_id_type=MESH)

    for d in (-1, 1):
        signal(barrier, chan_peer(d))
        signal(barrier, z_peer(d))
    signal(barrier, {"win": z * 2 + 1 - c})

    loads = [pltpu.make_async_copy(traces.at[0, b], raw.at[b], load_sem.at[b]) for b in range(B)]
    for copy in loads:
        copy.start()

    for h in range(2):
        bbuf[256 * h + 4 * CH : 256 * (h + 1), :] = jnp.zeros((256 - 4 * CH, K), BF16)
    for copy in loads:
        copy.wait()

    def y_copy(side, s):
        dst = yrecv[s].at[side]
        peer = lax.rem(p + (n_chan - 1 if side == 0 else 1), n_chan)
        return pltpu.make_async_remote_copy(
            src_ref=ysend.at[side, s], dst_ref=dst,
            send_sem=ys_sem.at[side, s], recv_sem=yr_sem.at[side, s],
            device_id={"chan": peer}, device_id_type=MESH,
        )

    for s in range(n):
        for side in range(2):
            block = tab[side * N_MAX + s]
            for g in range(0, CH, 16):
                ysend[side, s, g : g + 16, :] = whiten(raw[block, g : g + 16, :])
            if s == 0 and side == 0:
                pl.semaphore_wait(barrier, 5)
            y_copy(side, s).start()
            if s == 0 and side == 1:
                for d in (-1, 1):
                    signal(z_in.at[0], z_peer(d))
                    signal(chan_in.at[0], chan_peer(d))
            if s == n - 1 and side == 1:
                pl.semaphore_wait(z_in.at[0], 2)
                pl.semaphore_wait(chan_in.at[0], 2)
                for d in (-2, 2):
                    signal(z_in.at[1], z_peer(d))
                    signal(chan_in.at[1], chan_peer(d))

    for s in range(S):
        block = tab[HERE + s]
        for g in range(0, CH, 16):
            mine[s, g : g + 16, :] = whiten(raw[block, g : g + 16, :])

    zeros = jnp.zeros((16, K - TS), BF16)
    low = lax.broadcasted_iota(jnp.int32, (half, 128), 1) < 64

    def fold(C, write):
        for zz in range(n_z):
            top = C[zz * CH : zz * CH + half, :]
            bottom = C[zz * CH + half : (zz + 1) * CH, :]
            r0 = pltpu.roll(bottom[:, 0:128], 64, 1)
            r1 = pltpu.roll(bottom[:, 128:256], 64, 1)
            write(zz, 0, top[:, 0:128])
            write(zz, 1, jnp.where(low, top[:, 128:256], r0))
            write(zz, 2, jnp.where(low, r0, r1))

    def dot():
        return lax.dot_general(
            abuf[...], bbuf[...], (((1,), (1,)), ((), ())), preferred_element_type=F32
        )

    def x_copy(s):
        return pltpu.make_async_remote_copy(
            src_ref=xsend.at[s], dst_ref=xrecv.at[s],
            send_sem=xs_sem.at[s], recv_sem=xr_sem.at[s],
            device_id={"win": z * 2 + 1 - c}, device_id_type=MESH,
        )

    def z_copy(s, d):
        peer = lax.rem(z + d, n_z)
        return pltpu.make_async_remote_copy(
            src_ref=zsend.at[s, peer], dst_ref=zrecv.at[s, d],
            send_sem=zs_sem.at[s, d], recv_sem=zr_sem.at[s, d],
            device_id={"win": peer * 2 + c}, device_id_type=MESH,
        )

    def f_copy(s, d):
        return pltpu.make_async_remote_copy(
            src_ref=fsend.at[s], dst_ref=frecv.at[d * S + s],
            send_sem=fs_sem.at[s, d], recv_sem=fr_sem.at[s, d],
            device_id={"chan": lax.rem(p + d, n_chan)}, device_id_type=MESH,
        )

    def join(s):
        x_copy(s).wait_recv()
        for zz in range(n_z):
            zsend[s, zz] = (acc[zz] + xrecv[s, zz].astype(F32)).astype(BF16)
        own[s] = acc[z] + xrecv[s, z].astype(F32)

        @pl.when(s == 0)
        def _():
            pl.semaphore_wait(z_in.at[1], 2)

        for d in DIRECT:
            z_copy(s, d).start()

    def finish(s):
        if s == 0:
            pl.semaphore_wait(chan_in.at[2], 2)
        total = own[s]
        for d in DIRECT:
            z_copy(s, d).wait_recv()
            total = total + zrecv[s, d].astype(F32)
        total = total.astype(BF16)
        fsend[s] = total
        for d in range(1, n_chan):
            f_copy(s, d).start()
        frecv[s] = total

    @pl.loop(0, S)
    def _(s):
        for side in range(2):

            @pl.when(s == side)
            def _():
                y_copy(side, 0).wait_recv()
                other[...] = yrecv[0][side]

        for t in range(1, n):

            @pl.when(s == t + 1)
            def _():
                for side in range(2):
                    y_copy(side, t).wait_recv()

            @pl.when(s == t + 1 if t < n - 1 else s > t)
            def _():
                order = tab[OTHER + s] // 2
                side = 1 - tab[OTHER + s] % 2
                for g in range(0, CH, 16):
                    value = yrecv[1][side, g : g + 16, :]
                    for u in range(2, t + 1):
                        value = jnp.where(order == u, yrecv[u][side, g : g + 16, :], value)
                    other[g : g + 16, :] = value

        for late, early in FINISH[S]:

            @pl.when(s == late)
            def _():
                finish(early)

        is_left = jnp.where(s < 2, 1 - s, tab[OTHER + s] % 2) == 1
        for g in range(0, CH, 16):
            ours = mine[s, g : g + 16, :]
            theirs = other[g : g + 16, :]
            left = jnp.where(is_left, ours, theirs)
            right = jnp.where(is_left, theirs, ours)
            left = jnp.concatenate([left, zeros], axis=1)
            right = jnp.concatenate([right, zeros], axis=1)
            for zz in range(n_z):
                row = zz * CH + g
                abuf[row : row + 16, :] = pltpu.roll(left, (8 * zz - 32) % K, 1)
            for u in range(8):
                at = pl.multiple_of((1 - c if u < 4 else c) * 256, 256)
                bbuf[pl.ds(at + (u % 4) * CH + g, 16), :] = pltpu.roll(right, (-u) % K, 1)

        def write_send(zz, t, value):
            xsend[s, zz, :, t * 128 : (t + 1) * 128] = value.astype(BF16)

        def write_acc(zz, t, value):
            acc[zz, :, t * 128 : (t + 1) * 128] = value

        both = dot()
        theirs_half, ours_half = both[:, :256], both[:, 256:]
        fold(theirs_half, write_send)
        x_copy(s).start()

        @pl.when(s == 0)
        def _():
            pl.semaphore_wait(chan_in.at[1], 2)
            for d in (-4, 4):
                signal(chan_in.at[2], chan_peer(d))

        fold(ours_half, write_acc)
        join(s)

    done = [early for _, early in FINISH[S]]
    for s in range(S):
        if s not in done:
            finish(s)

    for s in range(n):
        for side in range(2):
            y_copy(side, s).wait_send()
    for s in range(S):
        x_copy(s).wait_send()
        for d in DIRECT:
            z_copy(s, d).wait_send()
        for d in range(1, n_chan):
            f_copy(s, d).wait_send()
    for s in range(S):
        for d in range(1, n_chan):
            f_copy(s, d).wait_recv()
    for k in range(P_CAP):
        out[k] = frecv[tab[SOURCE + k]].astype(F32) * (tab[LIVE + k].astype(F32) * scale)


def table_kernel(B, n_chan, blocks, pair_count, tab, tier, counts, lefts):
    p = lax.axis_index("chan")
    for e in range(n_chan + 4):
        counts[e] = 0
        lefts[e] = 0
    for t in range(TAB):
        tab[t] = 0
    starts = [blocks[0, P_CAP * o] // B for o in range(n_chan)]
    lives = [pair_count[o] for o in range(n_chan)]
    for start, live in zip(starts, lives):
        counts[start] = counts[start] + 1
        counts[start + live] = counts[start + live] - 1
    rights = [0] * len(TIERS)
    fits = [True] * len(TIERS)
    split = [[] for _ in TIERS]
    count = 0
    for e in range(n_chan):
        count = count + counts[e]
        for t, (n, S) in enumerate(TIERS):
            right = jnp.maximum(rights[t], 1)
            left = jnp.minimum(jnp.minimum(n, count), S - right)
            split[t].append(left)
            fit = jnp.logical_and(jnp.maximum(left, 1) + right <= S, count - left <= n)
            fits[t] = jnp.logical_and(fits[t], fit)
            rights[t] = count - left
    choice = jnp.int32(len(TIERS))
    S = jnp.int32(TIERS[-1][1])
    for t in reversed(range(len(TIERS))):
        choice = jnp.where(fits[t], t, choice)
        S = jnp.where(fits[t], TIERS[t][1], S)
    for e in range(n_chan):
        left = split[-1][e]
        for t in reversed(range(len(TIERS))):
            left = jnp.where(fits[t], split[t][e], left)
        lefts[e + 1] = left
    tier[0] = choice

    ranks = [0, 0]
    left_of = [lefts[p], lefts[p + 1]]
    rest_of_right = jnp.maximum(left_of[1], 1)
    for o, (start, live) in enumerate(zip(starts, lives)):
        for end in range(2):
            k = p - 1 + end - start
            here = jnp.logical_and(k >= 0, k < live)
            row = P_CAP * o + jnp.minimum(jnp.maximum(k, 0), P_CAP - 1)
            block = blocks[1 - end, row] - p * B
            rank = ranks[end]
            ranks[end] = rank + here.astype(jnp.int32)
            is_left = rank < left_of[end]
            order = jnp.where(is_left, rank, rank - left_of[end])
            if end == 0:
                works = jnp.logical_not(is_left)
                slot = jnp.where(order == 0, 1, rest_of_right + order)
            else:
                works = is_left
                slot = jnp.where(order == 0, 0, 1 + order)
            place = jnp.where(works, HERE + slot, end * N_MAX + order)
            tab[jnp.where(here, place, TRASH)] = block
            tab[jnp.where(jnp.logical_and(here, works), OTHER + slot, TRASH)] = 2 * order + end

    own_start = blocks[0, P_CAP * p] // B
    own_live = pair_count[p]
    for k in range(P_CAP):
        edge = own_start + k
        rank = 0
        for o, (start, live) in enumerate(zip(starts, lives)):
            inside = jnp.logical_and(edge >= start, edge < start + live)
            rank = rank + jnp.logical_and(inside, o < p).astype(jnp.int32)
        left = lefts[edge + 1]
        is_left = rank < left
        order = jnp.where(is_left, rank, rank - left)
        rest = jnp.where(is_left, 1, jnp.maximum(lefts[edge + 2], 1)) + order
        slot = jnp.where(order == 0, jnp.where(is_left, 0, 1), rest)
        away = p - jnp.where(is_left, edge, edge + 1)
        away = jnp.where(away < 0, away + n_chan, away)
        live = k < own_live
        tab[SOURCE + k] = jnp.where(live, away * S + slot, 0)
        tab[LIVE + k] = live.astype(jnp.int32)


def fast_path(tier, traces, tab):
    n, S = TIERS[tier]
    n_chan = lax.axis_size("chan")
    n_win = lax.axis_size("win")
    n_z = n_win // 2
    _, B, CH, TS = traces.shape
    K = TS + 128
    half = CH // 2

    dma = pltpu.SemaphoreType.DMA
    result = pl.pallas_call(
        functools.partial(kernel, n, S, 1.0 / math.sqrt(TS * n_win)),
        out_shape=jax.ShapeDtypeStruct((P_CAP, half, 8 * CH), F32),
        in_specs=[
            pl.BlockSpec(memory_space=pltpu.SMEM),
            pl.BlockSpec(memory_space=pl.ANY),
        ],
        out_specs=pl.BlockSpec(memory_space=pltpu.VMEM),
        scratch_shapes=[
            pltpu.VMEM((B, CH, TS), F32),
            pltpu.VMEM((n_z * CH, K), BF16),
            pltpu.VMEM((512, K), BF16),
            pltpu.VMEM((2, n, CH, TS), BF16),
            pltpu.VMEM((S, CH, TS), BF16),
            pltpu.VMEM((CH, TS), BF16),
            pltpu.VMEM((S, n_z, half, 8 * CH), BF16),
            pltpu.VMEM((S, n_z, half, 8 * CH), BF16),
            pltpu.VMEM((n_z, half, 8 * CH), F32),
            pltpu.VMEM((S, n_z, half, 8 * CH), BF16),
            pltpu.VMEM((S, n_z, half, 8 * CH), BF16),
            pltpu.VMEM((S, half, 8 * CH), F32),
            pltpu.VMEM((S, half, 8 * CH), BF16),
            pltpu.VMEM((n_chan * S, half, 8 * CH), BF16),
            dma((B,)),
            dma((2, n)), dma((2, n)),
            dma((S,)), dma((S,)),
            dma((S, n_z)), dma((S, n_z)),
            dma((S, n_chan)), dma((S, n_chan)),
            pltpu.SemaphoreType.REGULAR((2,)), pltpu.SemaphoreType.REGULAR((3,)),
        ]
        + [pltpu.VMEM((2, CH, TS), BF16)] * n,
        compiler_params=pltpu.CompilerParams(collective_id=tier, has_side_effects=True),
        name=f"stack_pairs_{n}_{S}",
    )(tab, traces)
    result = result.reshape(P_CAP, half, 2, 4, CH)
    return jnp.transpose(result, (3, 0, 2, 1, 4)).reshape(4, P_CAP, CH * CH)


def per_device(traces, pair_blocks, pair_count):
    n_chan = lax.axis_size("chan")
    smem = pl.BlockSpec(memory_space=pltpu.SMEM)
    tab, tier = pl.pallas_call(
        functools.partial(table_kernel, traces.shape[1], n_chan),
        out_shape=(jax.ShapeDtypeStruct((TAB,), jnp.int32), jax.ShapeDtypeStruct((1,), jnp.int32)),
        in_specs=[smem, smem],
        out_specs=(smem, smem),
        scratch_shapes=[pltpu.SMEM((n_chan + 4,), jnp.int32)] * 2,
        name="pair_tables",
    )(pair_blocks.T, pair_count)
    branches = [
        functools.partial(lambda tier, t, tab, pb, pc: fast_path(tier, t, tab), tier)
        for tier in range(len(TIERS))
    ]
    branches.append(lambda t, tab, pb, pc: general_path(t, pb, pc))
    return lax.switch(tier.reshape(()), branches, traces, tab, pair_blocks, pair_count)


def solution(mesh):
    in_specs = (P("win", "chan", None, None), P(), P())
    out_specs = P("win", "chan", None)
    return jax.shard_map(
        per_device, mesh=mesh, in_specs=in_specs, out_specs=out_specs, check_vma=False
    )
```
